512 devices in a mesh: half: 2 (over x_hi), quarter: 2 (over x_lo), grp: 128 (over y, z, core).
Axes of the slice: x: 4 (x_hi: 2, x_lo: 2; x = x_hi * 2 + x_lo), y: 4, z: 16, core: 2. Of those that a mesh axis runs over, the one named last changes fastest.
Arguments:
- rhs: float32 [131072, 512], P(('half', 'quarter', 'grp')), may hold values from -6 to 6
- left_one: float32 [131072, 128], P(('half', 'quarter', 'grp')), may hold values from -0.5 to 0.5
- left_two: float32 [131072, 128], P(('half', 'quarter', 'grp')), may hold values from -0.5 to 0.5
- middle_one: float32 [2, 128, 128, 128], P('half', 'grp'), may hold values from -0.5 to 0.5
- middle_two: float32 [4, 128, 128, 128], P(('half', 'quarter'), 'grp'), may hold values from -0.5 to 0.5
- right_one: float32 [131072, 128], P(('half', 'quarter', 'grp')), may hold values from -0.25 to 0.25
- right_two: float32 [131072, 128], P(('half', 'quarter', 'grp')), may hold values from -0.375 to 0.375
- order_one: int32 [2, 128, 128], P('half', 'grp'), may hold values from 0 to 127, each once within a row
- order_two: int32 [4, 128, 128], P(('half', 'quarter'), 'grp'), may hold values from 0 to 127, each once within a row
Outputs:
- product: float32 [131072, 512], P(('half', 'quarter', 'grp'))
The draws below stay inside these ranges and needn't reach their ends.
Inputs may be any that keep to these rules, and one draw needn't show every extreme that they name: `order_one`: each row along the last dimension is a permutation of 0 .. 127. `order_two`: each row along the last dimension is a permutation of 0 .. 127.
All inputs are finite; a program needn't handle non-finite values.
Results may differ from the reference program's by a relative error of at most 0.000071.
Values sent between devices are 32-bit elements; how exact they have to be, the bound alone decides.
A program may use at most 64 MiB of HBM per device.

```python
import jax
import jax.numpy as jnp
from jax import lax

CR = 256
NRHS = 512
RK = 128
NTOTAL = 131072
N_GRP = 128


def block_levels(stream_key, dims, split, least, largest):
    factor_of = 1.0
    for position, blocks in split:
        heights = jax.random.uniform(jax.random.fold_in(jax.random.fold_in(stream_key, 6), position), (blocks,), jnp.float32, least / len(split), largest / len(split))
        factor_of = factor_of * jnp.repeat(jnp.exp(heights), dims[position] // blocks).reshape((-1,) + (1,) * (len(dims) - 1 - position))
    return factor_of


def scatter_about(stream_key, dims, spread, limit, shards=(), dtype=jnp.bfloat16):
    values = jax.random.normal(stream_key, dims, jnp.float32) * spread
    if len(shards) > 0:
        values = block_levels(stream_key, dims, shards, -0.22, 0.18) * values
    return jnp.clip(values, min=-limit, max=limit).astype(dtype)


def setup_inputs(seed: int = 0) -> dict:
    seeds = jax.random.split(jax.random.key(seed), 10)
    return {
        "rhs": scatter_about(seeds[0], (NTOTAL, NRHS), 1.0, 6.0, ((0, 512),), jnp.float32),
        "left_one": scatter_about(seeds[1], (NTOTAL, RK), RK ** -0.5, 0.5, ((0, 512),), jnp.float32),
        "left_two": scatter_about(seeds[2], (NTOTAL, RK), RK ** -0.5, 0.5, ((0, 512),), jnp.float32),
        "middle_one": scatter_about(seeds[3], (2, N_GRP, RK, RK), RK ** -0.5, 0.5, ((0, 2), (1, 128)), jnp.float32),
        "middle_two": scatter_about(seeds[4], (4, N_GRP, RK, RK), RK ** -0.5, 0.5, ((0, 4), (1, 128)), jnp.float32),
        "right_one": scatter_about(seeds[5], (NTOTAL, RK), (2 * CR) ** -0.5, 0.25, ((0, 512),), jnp.float32),
        "right_two": scatter_about(seeds[6], (NTOTAL, RK), CR ** -0.5, 0.375, ((0, 512),), jnp.float32),
        "order_one": jax.vmap(lambda own: jax.random.permutation(own, N_GRP))(jax.random.split(seeds[7], 2 * N_GRP)).reshape((2, N_GRP, N_GRP)).astype(jnp.int32),
        "order_two": jax.vmap(lambda own: jax.random.permutation(own, N_GRP))(jax.random.split(seeds[8], 4 * N_GRP)).reshape((4, N_GRP, N_GRP)).astype(jnp.int32),
    }


def regroup(coeffs, order):
    groups = N_GRP
    part = RK // groups
    lead = coeffs.shape[:-2]
    parts = coeffs.reshape(lead + (groups, part, NRHS))
    inverse = jnp.argsort(order, axis=-1).astype(jnp.int32)
    index = jnp.broadcast_to(inverse[..., None, None], parts.shape)
    picked = jnp.take_along_axis(parts, index, axis=-3)
    moved = jnp.swapaxes(picked, -4, -3)
    return moved.reshape(coeffs.shape)


def reference(rhs, left_one, left_two, middle_one, middle_two, right_one, right_two, order_one, order_two):
    highest = lax.Precision.HIGHEST
    groups = N_GRP
    blocks = rhs.reshape(2, 2, groups, CR, NRHS)
    coeff_two = jnp.einsum('abgrk,abgrn->abgkn', right_two.reshape(2, 2, groups, CR, RK), blocks, precision=highest)
    moved_two = regroup(coeff_two, order_two.reshape(2, 2, groups, groups))[:, ::-1]
    mixed_two = jnp.einsum('abgkl,abgln->abgkn', middle_two.reshape(2, 2, groups, RK, RK), moved_two, precision=highest)
    result_two = jnp.einsum('abgrk,abgkn->abgrn', left_two.reshape(2, 2, groups, CR, RK), mixed_two, precision=highest)
    coeff_one = jnp.einsum('aqgrk,aqgrn->agkn', right_one.reshape(2, 2, groups, CR, RK), blocks, precision=highest)
    moved_one = regroup(coeff_one, order_one)[::-1]
    mixed_one = jnp.einsum('agkl,agln->agkn', middle_one, moved_one, precision=highest)
    result_one = jnp.einsum('aqgrk,agkn->aqgrn', left_one.reshape(2, 2, groups, CR, RK), mixed_one, precision=highest)
    return (result_one + result_two).reshape(NTOTAL, NRHS)
```

```python
import functools

import jax
import jax.numpy as jnp
from jax import lax
from jax.experimental import pallas as pl
from jax.experimental.pallas import tpu as pltpu
from jax.sharding import PartitionSpec as P

MESH = pl.DeviceIdType.MESH
G = 128
HALF = 64
NZ = 16
NY = 4
BF = jnp.bfloat16
F32 = jnp.float32


def split(a):
    high = a.astype(BF)
    return high, (a - high.astype(F32)).astype(BF)


def dot(a, b, dims=(((1,), (0,)), ((), ()))):
    return lax.dot_general(a, b, dims, preferred_element_type=F32)


def dot3(a, b):
    (ah, al), (bh, bl) = a, b
    return dot(ah, bh) + (dot(ah, bl) + dot(al, bh))


def permuted(factor, order, slot):
    hot = (order == slot).astype(F32).astype(BF)
    high, low = split(factor)
    nt = (((1,), (1,)), ((), ()))
    return dot(hot, high, nt).astype(BF), dot(hot, low, nt).astype(BF)


def kernel(
    x_hbm, l1_hbm, l2_hbm, m1_hbm, m2_hbm, rr1_hbm, rr2_hbm, o1_hbm, o2_hbm, out_hbm,
    x, l1, l2, m1, m2, rr1, rr2, o1, o2, out,
    s2, p1, in1, s1, r2, r1,
    load_sem, send2, recv2, xs, xr, send1, recv1, fs, fr, out_sem, stage_b, stage_c,
):
    h = lax.axis_index("half")
    q = lax.axis_index("quarter")
    me = lax.axis_index("grp")
    y, z, c = me // (2 * NZ), (me // 2) % NZ, me % 2

    loads = []
    for n, (a, b) in enumerate((
        (x_hbm, x), (rr2_hbm, rr2), (o2_hbm.at[0], o2), (rr1_hbm, rr1), (o1_hbm.at[0], o1),
        (m2_hbm.at[0, 0], m2), (m1_hbm.at[0, 0], m1), (l2_hbm, l2), (l1_hbm, l1),
    )):
        loads.append(pltpu.make_async_copy(a, b, load_sem.at[n]))

    def plane(s):
        t = (y * 2 + c + s) % (2 * NY)
        return {"half": h, "quarter": q, "grp": ((t // 2) * NZ + z) * 2 + t % 2}

    def across(s):
        t = (h * 2 + q) ^ s
        return {"half": t // 2, "quarter": t % 2, "grp": me}

    def column(s):
        return {"half": h, "quarter": q, "grp": (y * NZ + (z + s) % NZ) * 2 + c}

    barrier = pltpu.get_barrier_semaphore()
    for s in range(1, NZ):
        pl.semaphore_signal(barrier, inc=1, device_id=column(s), device_id_type=MESH)
    for s in range(1, 2 * NY):
        pl.semaphore_signal(barrier, inc=1, device_id=plane(s), device_id_type=MESH)
    for s in range(1, 4):
        pl.semaphore_signal(barrier, inc=1, device_id=across(s), device_id_type=MESH)
    for copy in loads:
        copy.start()

    slot2 = lax.broadcasted_iota(jnp.int32, (G, G), 0)
    slot1 = (slot2 % HALF) * 2 + slot2 // HALF
    loads[0].wait()
    xs_ = split(x[...])
    loads[1].wait()
    loads[2].wait()
    c2 = dot3(permuted(rr2[...], o2[...], slot2), xs_)
    for k in range(4):
        s2[:, k, :] = c2[:, 128 * k : 128 * k + 128]
    loads[3].wait()
    loads[4].wait()
    c1 = dot3(permuted(rr1[...], o1[...], slot1), xs_)
    for e in range(2):
        for k in range(4):
            p1[e, :, k, :] = c1[HALF * e : HALF * e + HALF, 128 * k : 128 * k + 128]

    pl.semaphore_wait(barrier, (NZ - 1) + (2 * NY - 1) + 3)
    for s in range(1, 2 * NY):
        pl.semaphore_signal(stage_b, inc=1, device_id=plane(s), device_id_type=MESH)
    part = pltpu.make_async_remote_copy(
        p1.at[1 - q], in1, xs, xr, device_id=across(1), device_id_type=MESH)
    part.start()
    pl.semaphore_wait(stage_b, 2 * NY - 1)
    for s in range(1, 4):
        pl.semaphore_signal(stage_c, inc=1, device_id=across(s), device_id_type=MESH)
    pl.semaphore_wait(stage_c, 3)

    def level_two(s, carry):
        d = (me + s) % G
        pltpu.make_async_remote_copy(
            s2.at[d], r2.at[me], send2, recv2,
            device_id={"half": h, "quarter": 1 - q, "grp": d}, device_id_type=MESH).start()
        return carry

    lax.fori_loop(0, 48, level_two, 0)

    part.wait()
    s1[...] = p1[q] + in1[...]

    def level_one(s, carry):
        k = (me // 2 + s) % HALF
        pltpu.make_async_remote_copy(
            s1.at[k], r1.at[me], send1, recv1,
            device_id={"half": 1 - h, "quarter": 1 - q, "grp": k * 2 + q}, device_id_type=MESH).start()
        return carry

    lax.fori_loop(0, HALF, level_one, 0)
    lax.fori_loop(48, G, level_two, 0)

    for copy in loads[5:]:
        copy.wait()
    m2s, m1s, l2s, l1s = split(m2[...]), split(m1[...]), split(l2[...]), split(l1[...])

    first = c == 1 - q
    forward = pltpu.make_async_remote_copy(
        r1, r1, fs, fr, device_id=across(1), device_id_type=MESH)
    rows1 = pltpu.make_async_remote_copy(
        r1, r1, send1, recv1, device_id=across(1), device_id_type=MESH)
    rows2 = pltpu.make_async_remote_copy(
        s2, r2, send2, recv2, device_id=across(1), device_id_type=MESH)
    sent1 = pltpu.make_async_remote_copy(
        s1, s1, send1, recv1, device_id=across(1), device_id_type=MESH)

    @pl.when(first)
    def _():
        rows1.wait_recv()
        forward.start()

    rows2.wait_recv()
    parts = []
    for k in range(4):
        w2 = split(dot3(m2s, split(r2[:, k, :])))
        parts.append(dot3(l2s, w2))

    @pl.when(jnp.logical_not(first))
    def _():
        forward.wait_recv()

    stores = []
    for k in range(4):
        w1 = split(dot3(m1s, split(r1[:, k, :])))
        out[:, 128 * k : 128 * k + 128] = parts[k] + dot3(l1s, w1)
    store = pltpu.make_async_copy(out, out_hbm, out_sem)
    store.start()

    @pl.when(first)
    def _():
        forward.wait_send()

    rows2.wait_send()
    sent1.wait_send()
    store.wait()


def on_device(rhs, left_one, left_two, middle_one, middle_two, right_one, right_two, order_one, order_two):
    dma = pltpu.SemaphoreType.DMA
    any_space = pl.BlockSpec(memory_space=pl.ANY)
    return pl.pallas_call(
        kernel,
        out_shape=jax.ShapeDtypeStruct((256, 512), F32),
        in_specs=[any_space] * 9,
        out_specs=any_space,
        scratch_shapes=[
            pltpu.VMEM((256, 512), F32),
            pltpu.VMEM((256, 128), F32),
            pltpu.VMEM((256, 128), F32),
            pltpu.VMEM((128, 128), F32),
            pltpu.VMEM((128, 128), F32),
            pltpu.VMEM((256, 128), F32),
            pltpu.VMEM((256, 128), F32),
            pltpu.VMEM((1, 128), jnp.int32),
            pltpu.VMEM((1, 128), jnp.int32),
            pltpu.VMEM((256, 512), F32),
            pltpu.VMEM((G, 4, 128), F32),
            pltpu.VMEM((2, HALF, 4, 128), F32),
            pltpu.VMEM((HALF, 4, 128), F32),
            pltpu.VMEM((HALF, 4, 128), F32),
            pltpu.VMEM((G, 4, 128), F32),
            pltpu.VMEM((G, 4, 128), F32),
            dma((9,)), dma, dma, dma, dma, dma, dma, dma, dma, dma,
            pltpu.SemaphoreType.REGULAR,
            pltpu.SemaphoreType.REGULAR,
        ],
        compiler_params=pltpu.CompilerParams(collective_id=0, has_side_effects=True),
        name="butterfly",
    )(rhs, left_one, left_two, middle_one, middle_two, right_one, right_two, order_one, order_two)


def solution(mesh):
    rows = P(("half", "quarter", "grp"), None)
    in_specs = (
        rows, rows, rows,
        P("half", "grp", None, None),
        P(("half", "quarter"), "grp", None, None),
        rows, rows,
        P("half", "grp", None),
        P(("half", "quarter"), "grp", None),
    )
    return jax.shard_map(on_device, mesh=mesh, in_specs=in_specs, out_specs=rows, check_vma=False)
```

```python
import functools

import jax
import jax.numpy as jnp
from jax import lax
from jax.experimental import pallas as pl
from jax.experimental.pallas import tpu as pltpu
from jax.sharding import PartitionSpec as P

MESH = pl.DeviceIdType.MESH
G = 128
HALF = 64
NZ = 16
NY = 4
BF = jnp.bfloat16
F32 = jnp.float32


def split(a):
    high = a.astype(BF)
    return high, (a - high.astype(F32)).astype(BF)


def dot(a, b, dims=(((1,), (0,)), ((), ()))):
    return lax.dot_general(a, b, dims, preferred_element_type=F32)


def dot3(a, b):
    (ah, al), (bh, bl) = a, b
    return dot(ah, bh) + (dot(ah, bl) + dot(al, bh))


def permuted(factor, order, slot):
    hot = (order == slot).astype(F32).astype(BF)
    high, low = split(factor)
    nt = (((1,), (1,)), ((), ()))
    return dot(hot, high, nt).astype(BF), dot(hot, low, nt).astype(BF)


NEAR = (4, -4, 3, -3, 2, -2, 1, -1)
FAR = (8, 7, -7, 6, -6, 5, -5)


def kernel(
    x_hbm, l1_hbm, l2_hbm, m1_hbm, m2_hbm, rr1_hbm, rr2_hbm, o1_hbm, o2_hbm, out,
    x, l1, l2, m1, m2, rr1, rr2, o1, o2,
    s2, p1, in1, s1, z2, r2, r1,
    load_sem, zs2, zr2, xs, xr, zs1, zr1, send2, recv2, fs, fr, stage, opposite_in,
):
    h = lax.axis_index("half")
    q = lax.axis_index("quarter")
    me = lax.axis_index("grp")
    y, z, c = me // (2 * NZ), (me // 2) % NZ, me % 2
    yc = y * 2 + c

    loads = []
    for n, (a, b) in enumerate((
        (x_hbm, x), (rr2_hbm, rr2), (o2_hbm.at[0], o2), (rr1_hbm, rr1), (o1_hbm.at[0], o1),
        (m2_hbm.at[0, 0], m2), (m1_hbm.at[0, 0], m1), (l2_hbm, l2), (l1_hbm, l1),
    )):
        loads.append(pltpu.make_async_copy(a, b, load_sem.at[n]))

    def signal(semaphore, device):
        pl.semaphore_signal(semaphore, inc=1, device_id=device, device_id_type=MESH)

    def place(zz, t):
        return ((t // 2) * NZ + zz) * 2 + t % 2

    def level(dz):
        return (z + dz + NZ) % NZ

    def column(dz):
        return {"half": h, "quarter": q, "grp": place(level(dz), yc)}

    def sibling(dz):
        return {"half": h, "quarter": 1 - q, "grp": place(level(dz), yc)}

    across = {"half": h, "quarter": 1 - q, "grp": me}
    opposite = {"half": 1 - h, "quarter": q, "grp": me}

    for copy in loads:
        copy.start()
    barrier = pltpu.get_barrier_semaphore()
    for dz in NEAR:
        signal(barrier, sibling(dz))
    for dz in (4, -4):
        signal(barrier, column(dz))
    signal(barrier, opposite)
    for s in range(1, 16):
        t = (yc * 2 + q + s) % 16
        signal(barrier, {"half": h, "quarter": t % 2, "grp": place(z, t // 2)})

    i = lax.broadcasted_iota(jnp.int32, (G, G), 0)
    slot2 = (((i // 2) % 4) * NZ + i // 8) * 2 + i % 2
    slot1 = ((i // 32) * NZ + i % NZ) * 2 + (i // NZ) % 2
    loads[0].wait()
    xs_ = split(x[...])
    loads[1].wait()
    loads[2].wait()
    c2 = dot3(permuted(rr2[...], o2[...], slot2), xs_)
    for k in range(4):
        s2[:, k, :] = c2[:, 128 * k : 128 * k + 128]
    loads[3].wait()
    loads[4].wait()
    c1 = dot3(permuted(rr1[...], o1[...], slot1), xs_)
    for k in range(4):
        p1[:, k, :] = c1[:, 128 * k : 128 * k + 128]

    def along_two(dz):
        return pltpu.make_async_remote_copy(
            s2.at[pl.ds(level(dz) * 8, 8)], z2.at[-dz % NZ], zs2, zr2.at[-dz % NZ],
            device_id=sibling(dz), device_id_type=MESH)

    def spread_two(first, count):
        for zi in range(first, first + count):
            along_two(-zi).wait_recv()

        def send(n, carry):
            t = (yc + n) % 8
            pltpu.make_async_remote_copy(
                z2.at[pl.ds(first, count), t], r2.at[pl.ds(yc * NZ + first, count)], send2, recv2,
                device_id={"half": h, "quarter": q, "grp": place(z, t)}, device_id_type=MESH).start()
            return carry

        lax.fori_loop(1, 8, send, 0)

    alone = c == q

    def spread_one(n, carry):
        t = (yc + n) % 8
        pltpu.make_async_remote_copy(
            p1.at[pl.ds(t * NZ, NZ)], in1.at[q * 4 + y], xs, xr,
            device_id={"half": h, "quarter": c, "grp": place(z, t)}, device_id_type=MESH).start()
        return carry

    def along_one(dz):
        return pltpu.make_async_remote_copy(
            s1.at[:, level(dz)], r1.at[q, -dz % NZ], zs1, zr1.at[-dz % NZ],
            device_id={"half": 1 - h, "quarter": 1 - q, "grp": place(level(dz), yc)},
            device_id_type=MESH)

    def whole(a, b, sent, received):
        return pltpu.make_async_remote_copy(a, b, sent, received, device_id=across, device_id_type=MESH)

    def share(first, count):
        for zi in range(first, first + count):
            row = r1.at[1 - q, zi]
            whole(row, row, zs1, zr1.at[zi]).wait_recv()
        rows = r1.at[1 - q, pl.ds(first, count)]
        whole(rows, rows, fs, fr).start()

    pl.semaphore_wait(barrier, 8 + 2 + 1 + 15)
    for dz in (4, -4):
        signal(stage, column(dz))

    @pl.when(jnp.logical_not(alone))
    def _():
        spread_one(0, 0)

    lax.fori_loop(1, 8, spread_one, 0)

    @pl.when(alone)
    def _():
        in1[q * 4 + y] = p1[pl.ds(yc * NZ, NZ)]

    for dz in NEAR[:4]:
        along_two(dz).start()
    pl.semaphore_wait(stage, 2)
    signal(opposite_in, opposite)
    for dz in FAR:
        along_two(dz).start()
    met = [whole(p1.at[pl.ds(0, NZ * n)], p1.at[pl.ds(0, NZ * n)], xs, xr) for n in (7, 8)]

    @pl.when(alone)
    def _():
        met[0].wait_recv()

    @pl.when(jnp.logical_not(alone))
    def _():
        met[1].wait_recv()

    s1[...] = in1[0:4] + in1[4:8]
    pl.semaphore_wait(opposite_in, 1)
    for dz in FAR + NEAR + (0,):
        along_one(dz).start()
    for dz in NEAR[4:] + (0,):
        along_two(dz).start()
    spread_two(12, 2)
    spread_two(3, 2)
    spread_two(7, 3)
    spread_two(5, 2)
    spread_two(10, 2)
    share(5, 7)
    share(12, 4)
    share(0, 5)
    spread_two(14, 2)
    spread_two(0, 3)
    r2[pl.ds(yc * NZ, NZ)] = z2[:, yc]

    for copy in loads[5:]:
        copy.wait()
    j = lax.broadcasted_iota(jnp.int32, (G, G), 1)
    hot2 = (((j // 32) * NZ + (z + j % NZ) % NZ) * 2 + (j // NZ) % 2 == i).astype(F32).astype(BF)
    hot1 = (((j % 4) * NZ + (z + (j // 4) % NZ) % NZ) * 2 + j // HALF == i).astype(F32).astype(BF)
    m2s = tuple(dot(v, hot2).astype(BF) for v in split(m2[...]))
    m1s = tuple(dot(v, hot1).astype(BF) for v in split(m1[...]))
    l2s, l1s = split(l2[...]), split(l1[...])

    rows2 = whole(r2.at[pl.ds(0, 7 * NZ)], r2.at[pl.ds(0, 7 * NZ)], send2, recv2)
    shared = whole(r1.at[q], r1.at[q], fs, fr)
    shared.wait_recv()
    for k in range(4):
        w1 = split(dot3(m1s, split(r1[:, :, :, k, :].reshape(G, 128))))
        out[:, 128 * k : 128 * k + 128] = dot3(l1s, w1)
    rows2.wait_recv()
    for k in range(4):
        w2 = split(dot3(m2s, split(r2[:, k, :])))
        out[:, 128 * k : 128 * k + 128] += dot3(l2s, w2)
    whole(s2, s2, zs2, zr2.at[0]).wait_send()
    whole(r1.at[0], r1.at[0], zs1, zr1.at[0]).wait_send()

    @pl.when(alone)
    def _():
        met[0].wait_send()

    @pl.when(jnp.logical_not(alone))
    def _():
        met[1].wait_send()

    rows2.wait_send()
    shared.wait_send()


def on_device(rhs, left_one, left_two, middle_one, middle_two, right_one, right_two, order_one, order_two):
    dma = pltpu.SemaphoreType.DMA
    any_space = pl.BlockSpec(memory_space=pl.ANY)
    return pl.pallas_call(
        kernel,
        out_shape=pltpu.VMEM((256, 512), F32),
        in_specs=[any_space] * 9,
        out_specs=pl.BlockSpec(memory_space=pltpu.VMEM),
        scratch_shapes=[
            pltpu.VMEM((256, 512), F32),
            pltpu.VMEM((256, 128), F32),
            pltpu.VMEM((256, 128), F32),
            pltpu.VMEM((128, 128), F32),
            pltpu.VMEM((128, 128), F32),
            pltpu.VMEM((256, 128), F32),
            pltpu.VMEM((256, 128), F32),
            pltpu.VMEM((1, 128), jnp.int32),
            pltpu.VMEM((1, 128), jnp.int32),
            pltpu.VMEM((G, 4, 128), F32),
            pltpu.VMEM((G, 4, 128), F32),
            pltpu.VMEM((8, NZ, 4, 128), F32),
            pltpu.VMEM((4, NZ, 4, 128), F32),
            pltpu.VMEM((NZ, 8, 4, 128), F32),
            pltpu.VMEM((G, 4, 128), F32),
            pltpu.VMEM((2, NZ, 4, 4, 128), F32),
            dma((9,)), dma, dma((NZ,)), dma, dma, dma, dma((NZ,)), dma, dma, dma, dma,
            pltpu.SemaphoreType.REGULAR,
            pltpu.SemaphoreType.REGULAR,
        ],
        compiler_params=pltpu.CompilerParams(collective_id=0, has_side_effects=True),
        name="butterfly",
    )(rhs, left_one, left_two, middle_one, middle_two, right_one, right_two, order_one, order_two)


def solution(mesh):
    rows = P(("half", "quarter", "grp"), None)
    in_specs = (
        rows, rows, rows,
        P("half", "grp", None, None),
        P(("half", "quarter"), "grp", None, None),
        rows, rows,
        P("half", "grp", None),
        P(("half", "quarter"), "grp", None),
    )
    return jax.shard_map(on_device, mesh=mesh, in_specs=in_specs, out_specs=rows, check_vma=False)
```

```python
import functools

import jax
import jax.numpy as jnp
from jax import lax
from jax.experimental import pallas as pl
from jax.experimental.pallas import tpu as pltpu
from jax.sharding import PartitionSpec as P

MESH = pl.DeviceIdType.MESH
G = 128
HALF = 64
NZ = 16
NY = 4
BF = jnp.bfloat16
F32 = jnp.float32


def split(a):
    high = a.astype(BF)
    return high, (a - high.astype(F32)).astype(BF)


def dot(a, b, dims=(((1,), (0,)), ((), ()))):
    return lax.dot_general(a, b, dims, preferred_element_type=F32)


def dot3(a, b):
    (ah, al), (bh, bl) = a, b
    return dot(ah, bh) + (dot(ah, bl) + dot(al, bh))


def deep3(a, b):
    (ah, al), (bh, bl) = a, b
    return dot(jnp.concatenate([ah, al], 1), jnp.concatenate([bh, bh], 0)) + dot(ah, bl)


def permuted(factor, order, slot):
    hot = (order == slot).astype(F32).astype(BF)
    high, low = split(factor)
    nt = (((1,), (1,)), ((), ()))
    return dot(hot, high, nt).astype(BF), dot(hot, low, nt).astype(BF)


NEAR = (4, -4, 3, -3, 2, -2, 1, -1)
FAR = (8, 7, -7, 6, -6, 5, -5)


def kernel(
    x_hbm, l1_hbm, l2_hbm, m1_hbm, m2_hbm, rr1_hbm, rr2_hbm, o1_hbm, o2_hbm, out,
    x, l1, l2, m1, m2, rr1, rr2, o1, o2,
    s2, p1, in1, s1, z2, r2, r1,
    load_sem, zs2, zr2, xs, xr, zs1, zr1, send2, recv2, fs, fr, stage, opposite_in,
):
    h = lax.axis_index("half")
    q = lax.axis_index("quarter")
    me = lax.axis_index("grp")
    y, z, c = me // (2 * NZ), (me // 2) % NZ, me % 2
    yc = y * 2 + c

    loads = []
    for n, (a, b) in enumerate((
        (x_hbm, x), (rr2_hbm, rr2), (o2_hbm.at[0], o2), (rr1_hbm, rr1), (o1_hbm.at[0], o1),
        (m2_hbm.at[0, 0], m2), (m1_hbm.at[0, 0], m1), (l2_hbm, l2), (l1_hbm, l1),
    )):
        loads.append(pltpu.make_async_copy(a, b, load_sem.at[n]))

    def signal(semaphore, device):
        pl.semaphore_signal(semaphore, inc=1, device_id=device, device_id_type=MESH)

    def place(zz, t):
        return ((t // 2) * NZ + zz) * 2 + t % 2

    def level(dz):
        return (z + dz + NZ) % NZ

    def column(dz):
        return {"half": h, "quarter": q, "grp": place(level(dz), yc)}

    def sibling(dz):
        return {"half": h, "quarter": 1 - q, "grp": place(level(dz), yc)}

    across = {"half": h, "quarter": 1 - q, "grp": me}
    opposite = {"half": 1 - h, "quarter": q, "grp": me}

    for copy in loads:
        copy.start()
    barrier = pltpu.get_barrier_semaphore()
    for dz in NEAR:
        signal(barrier, sibling(dz))
    for dz in (4, -4):
        signal(barrier, column(dz))
    signal(barrier, opposite)
    for s in range(1, 16):
        t = (yc * 2 + q + s) % 16
        signal(barrier, {"half": h, "quarter": t % 2, "grp": place(z, t // 2)})

    i = lax.broadcasted_iota(jnp.int32, (G, G), 0)
    slot2 = (((i // 2) % 4) * NZ + i // 8) * 2 + i % 2
    slot1 = ((i // 32) * NZ + i % NZ) * 2 + (i // NZ) % 2
    loads[0].wait()
    xs_ = split(x[...])
    loads[1].wait()
    loads[2].wait()
    c2 = dot3(permuted(rr2[...], o2[...], slot2), xs_)
    for k in range(4):
        s2[:, k, :] = c2[:, 128 * k : 128 * k + 128]
    loads[3].wait()
    loads[4].wait()
    c1 = dot3(permuted(rr1[...], o1[...], slot1), xs_)
    for k in range(4):
        p1[:, k, :] = c1[:, 128 * k : 128 * k + 128]

    def along_two(dz):
        return pltpu.make_async_remote_copy(
            s2.at[pl.ds(level(dz) * 8, 8)], z2.at[-dz % NZ], zs2, zr2.at[-dz % NZ],
            device_id=sibling(dz), device_id_type=MESH)

    def spread_two(first, count):
        for zi in range(first, first + count):
            along_two(-zi).wait_recv()

        def send(n, carry):
            t = (yc + n) % 8
            pltpu.make_async_remote_copy(
                z2.at[pl.ds(first, count), t], r2.at[pl.ds(yc * NZ + first, count)], send2, recv2,
                device_id={"half": h, "quarter": q, "grp": place(z, t)}, device_id_type=MESH).start()
            return carry

        lax.fori_loop(1, 8, send, 0)

    alone = c == q

    def spread_one(n, carry):
        t = (yc + n) % 8
        pltpu.make_async_remote_copy(
            p1.at[pl.ds(t * NZ, NZ)], in1.at[q * 4 + y], xs, xr,
            device_id={"half": h, "quarter": c, "grp": place(z, t)}, device_id_type=MESH).start()
        return carry

    def along_one(dz):
        return pltpu.make_async_remote_copy(
            s1.at[:, level(dz)], r1.at[q, -dz % NZ], zs1, zr1.at[-dz % NZ],
            device_id={"half": 1 - h, "quarter": 1 - q, "grp": place(level(dz), yc)},
            device_id_type=MESH)

    def whole(a, b, sent, received):
        return pltpu.make_async_remote_copy(a, b, sent, received, device_id=across, device_id_type=MESH)

    def share(first, count):
        for zi in range(first, first + count):
            row = r1.at[1 - q, zi]
            whole(row, row, zs1, zr1.at[zi]).wait_recv()
        rows = r1.at[1 - q, pl.ds(first, count)]
        whole(rows, rows, fs, fr).start()

    pl.semaphore_wait(barrier, 8 + 2 + 1 + 15)
    for dz in (4, -4):
        signal(stage, column(dz))

    @pl.when(jnp.logical_not(alone))
    def _():
        spread_one(0, 0)

    lax.fori_loop(1, 8, spread_one, 0)

    @pl.when(alone)
    def _():
        in1[q * 4 + y] = p1[pl.ds(yc * NZ, NZ)]

    for dz in NEAR + (0,):
        along_two(dz).start()
    pl.semaphore_wait(stage, 2)
    signal(opposite_in, opposite)
    for dz in FAR:
        along_two(dz).start()
    met = [whole(p1.at[pl.ds(0, NZ * n)], p1.at[pl.ds(0, NZ * n)], xs, xr) for n in (7, 8)]

    @pl.when(alone)
    def _():
        met[0].wait_recv()

    @pl.when(jnp.logical_not(alone))
    def _():
        met[1].wait_recv()

    s1[...] = in1[0:4] + in1[4:8]
    pl.semaphore_wait(opposite_in, 1)
    for dz in FAR + NEAR + (0,):
        along_one(dz).start()
    spread_two(12, 4)
    spread_two(0, 5)
    spread_two(7, 3)
    spread_two(5, 2)
    spread_two(10, 2)
    r2[pl.ds(yc * NZ, NZ)] = z2[:, yc]
    share(7, 3)
    share(5, 2)
    share(10, 2)
    share(12, 4)
    share(0, 5)

    for copy in loads[5:]:
        copy.wait()
    j = lax.broadcasted_iota(jnp.int32, (G, G), 1)
    hot2 = (((j // 32) * NZ + (z + j % NZ) % NZ) * 2 + (j // NZ) % 2 == i).astype(F32).astype(BF)
    hot1 = (((j % 4) * NZ + (z + (j // 4) % NZ) % NZ) * 2 + j // HALF == i).astype(F32).astype(BF)
    m2s = tuple(dot(v, hot2).astype(BF) for v in split(m2[...]))
    m1s = tuple(dot(v, hot1).astype(BF) for v in split(m1[...]))
    l2s, l1s = split(l2[...]), split(l1[...])

    rows2 = whole(r2.at[pl.ds(0, 7 * NZ)], r2.at[pl.ds(0, 7 * NZ)], send2, recv2)
    rows2.wait_recv()
    for k in (0, 2):
        rows = jnp.concatenate([r2[:, k, :], r2[:, k + 1, :]], 1)
        w2 = split(deep3(m2s, split(rows)))
        out[:, 128 * k : 128 * k + 256] = deep3(l2s, w2)
    shared = whole(r1.at[q], r1.at[q], fs, fr)
    shared.wait_recv()
    for k in (0, 2):
        rows = jnp.concatenate([r1[:, :, :, n, :].reshape(G, 128) for n in (k, k + 1)], 1)
        w1 = split(deep3(m1s, split(rows)))
        out[:, 128 * k : 128 * k + 256] += deep3(l1s, w1)
    whole(s2, s2, zs2, zr2.at[0]).wait_send()
    whole(r1.at[0], r1.at[0], zs1, zr1.at[0]).wait_send()

    @pl.when(alone)
    def _():
        met[0].wait_send()

    @pl.when(jnp.logical_not(alone))
    def _():
        met[1].wait_send()

    rows2.wait_send()
    shared.wait_send()


def on_device(rhs, left_one, left_two, middle_one, middle_two, right_one, right_two, order_one, order_two):
    dma = pltpu.SemaphoreType.DMA
    any_space = pl.BlockSpec(memory_space=pl.ANY)
    return pl.pallas_call(
        kernel,
        out_shape=pltpu.VMEM((256, 512), F32),
        in_specs=[any_space] * 9,
        out_specs=pl.BlockSpec(memory_space=pltpu.VMEM),
        scratch_shapes=[
            pltpu.VMEM((256, 512), F32),
            pltpu.VMEM((256, 128), F32),
            pltpu.VMEM((256, 128), F32),
            pltpu.VMEM((128, 128), F32),
            pltpu.VMEM((128, 128), F32),
            pltpu.VMEM((256, 128), F32),
            pltpu.VMEM((256, 128), F32),
            pltpu.VMEM((1, 128), jnp.int32),
            pltpu.VMEM((1, 128), jnp.int32),
            pltpu.VMEM((G, 4, 128), F32),
            pltpu.VMEM((G, 4, 128), F32),
            pltpu.VMEM((8, NZ, 4, 128), F32),
            pltpu.VMEM((4, NZ, 4, 128), F32),
            pltpu.VMEM((NZ, 8, 4, 128), F32),
            pltpu.VMEM((G, 4, 128), F32),
            pltpu.VMEM((2, NZ, 4, 4, 128), F32),
            dma((9,)), dma, dma((NZ,)), dma, dma, dma, dma((NZ,)), dma, dma, dma, dma,
            pltpu.SemaphoreType.REGULAR,
            pltpu.SemaphoreType.REGULAR,
        ],
        compiler_params=pltpu.CompilerParams(collective_id=0, has_side_effects=True),
        name="butterfly",
    )(rhs, left_one, left_two, middle_one, middle_two, right_one, right_two, order_one, order_two)


def solution(mesh):
    rows = P(("half", "quarter", "grp"), None)
    in_specs = (
        rows, rows, rows,
        P("half", "grp", None, None),
        P(("half", "quarter"), "grp", None, None),
        rows, rows,
        P("half", "grp", None),
        P(("half", "quarter"), "grp", None),
    )
    return jax.shard_map(on_device, mesh=mesh, in_specs=in_specs, out_specs=rows, check_vma=False)
```

```python
import functools

import jax
import jax.numpy as jnp
from jax import lax
from jax.experimental import pallas as pl
from jax.experimental.pallas import tpu as pltpu
from jax.sharding import PartitionSpec as P

MESH = pl.DeviceIdType.MESH
G = 128
HALF = 64
NZ = 16
NY = 4
BF = jnp.bfloat16
F32 = jnp.float32


def split(a):
    high = a.astype(BF)
    return high, (a - high.astype(F32)).astype(BF)


def dot(a, b, dims=(((1,), (0,)), ((), ()))):
    return lax.dot_general(a, b, dims, preferred_element_type=F32)


def dot3(a, b):
    (ah, al), (bh, bl) = a, b
    return dot(ah, bh) + (dot(ah, bl) + dot(al, bh))


def deep3(a, b):
    (ah, al), (bh, bl) = a, b
    return dot(jnp.concatenate([ah, al], 1), jnp.concatenate([bh, bh], 0)) + dot(ah, bl)


def permuted(factor, order, slot):
    hot = (order == slot).astype(F32).astype(BF)
    high, low = split(factor)
    nt = (((1,), (1,)), ((), ()))
    return dot(hot, high, nt).astype(BF), dot(hot, low, nt).astype(BF)


NEAR = (4, -4, 3, -3, 2, -2, 1, -1)
FAR = (8, 7, -7, 6, -6, 5, -5)


def kernel(
    x_hbm, l1_hbm, l2_hbm, m1_hbm, m2_hbm, rr1_hbm, rr2_hbm, o1_hbm, o2_hbm, out,
    x, l1, l2, m1, m2, rr1, rr2, o1, o2,
    s2, p1, in1, s1, z2, r2, r1,
    load_sem, zs2, zr2, xs, xr, zs1, zr1, send2, recv2, fs, fr, stage, opposite_in,
):
    h = lax.axis_index("half")
    q = lax.axis_index("quarter")
    me = lax.axis_index("grp")
    y, z, c = me // (2 * NZ), (me // 2) % NZ, me % 2
    yc = y * 2 + c

    loads = []
    for n, (a, b) in enumerate((
        (x_hbm, x), (rr2_hbm, rr2), (o2_hbm.at[0], o2), (rr1_hbm, rr1), (o1_hbm.at[0], o1),
        (m2_hbm.at[0, 0], m2), (m1_hbm.at[0, 0], m1), (l2_hbm, l2), (l1_hbm, l1),
    )):
        loads.append(pltpu.make_async_copy(a, b, load_sem.at[n]))

    def signal(semaphore, device):
        pl.semaphore_signal(semaphore, inc=1, device_id=device, device_id_type=MESH)

    def place(zz, t):
        return ((t // 2) * NZ + zz) * 2 + t % 2

    def level(dz):
        return (z + dz + NZ) % NZ

    def column(dz):
        return {"half": h, "quarter": q, "grp": place(level(dz), yc)}

    def sibling(dz):
        return {"half": h, "quarter": 1 - q, "grp": place(level(dz), yc)}

    across = {"half": h, "quarter": 1 - q, "grp": me}
    opposite = {"half": 1 - h, "quarter": q, "grp": me}

    for copy in loads:
        copy.start()
    barrier = pltpu.get_barrier_semaphore()
    for dz in NEAR:
        signal(barrier, sibling(dz))
    for dz in (4, -4):
        signal(barrier, column(dz))
    signal(barrier, opposite)
    for s in range(1, 16):
        t = (yc * 2 + q + s) % 16
        signal(barrier, {"half": h, "quarter": t % 2, "grp": place(z, t // 2)})

    i = lax.broadcasted_iota(jnp.int32, (G, G), 0)
    slot2 = (((i // 2) % 4) * NZ + i // 8) * 2 + i % 2
    slot1 = ((i // 32) * NZ + i % NZ) * 2 + (i // NZ) % 2
    loads[0].wait()
    xs_ = split(x[...])
    loads[1].wait()
    loads[2].wait()
    c2 = dot3(permuted(rr2[...], o2[...], slot2), xs_)
    for k in range(4):
        s2[:, k, :] = c2[:, 128 * k : 128 * k + 128]
    loads[3].wait()
    loads[4].wait()
    c1 = dot3(permuted(rr1[...], o1[...], slot1), xs_)
    for k in range(4):
        p1[:, k, :] = c1[:, 128 * k : 128 * k + 128]

    def along_two(dz):
        return pltpu.make_async_remote_copy(
            s2.at[pl.ds(level(dz) * 8, 8)], z2.at[-dz % NZ], zs2, zr2.at[-dz % NZ],
            device_id=sibling(dz), device_id_type=MESH)

    def spread_two(first, count):
        for zi in range(first, first + count):
            along_two(-zi).wait_recv()

        def send(n, carry):
            t = (yc + n) % 8
            pltpu.make_async_remote_copy(
                z2.at[pl.ds(first, count), t], r2.at[pl.ds(yc * NZ + first, count)], send2, recv2,
                device_id={"half": h, "quarter": q, "grp": place(z, t)}, device_id_type=MESH).start()
            return carry

        lax.fori_loop(1, 8, send, 0)

    alone = c == q

    def spread_one(n, carry):
        t = (yc + n) % 8
        pltpu.make_async_remote_copy(
            p1.at[pl.ds(t * NZ, NZ)], in1.at[q * 4 + y], xs, xr,
            device_id={"half": h, "quarter": c, "grp": place(z, t)}, device_id_type=MESH).start()
        return carry

    def along_one(dz):
        return pltpu.make_async_remote_copy(
            s1.at[:, level(dz)], r1.at[q, -dz % NZ], zs1, zr1.at[-dz % NZ],
            device_id={"half": 1 - h, "quarter": 1 - q, "grp": place(level(dz), yc)},
            device_id_type=MESH)

    def whole(a, b, sent, received):
        return pltpu.make_async_remote_copy(a, b, sent, received, device_id=across, device_id_type=MESH)

    def share(first, count):
        for zi in range(first, first + count):
            row = r1.at[1 - q, zi]
            whole(row, row, zs1, zr1.at[zi]).wait_recv()
        rows = r1.at[1 - q, pl.ds(first, count)]
        whole(rows, rows, fs, fr).start()

    pl.semaphore_wait(barrier, 8 + 2 + 1 + 15)
    for dz in (4, -4):
        signal(stage, column(dz))

    @pl.when(jnp.logical_not(alone))
    def _():
        spread_one(0, 0)

    lax.fori_loop(1, 8, spread_one, 0)

    @pl.when(alone)
    def _():
        in1[q * 4 + y] = p1[pl.ds(yc * NZ, NZ)]

    for dz in NEAR + (0,):
        along_two(dz).start()
    pl.semaphore_wait(stage, 2)
    signal(opposite_in, opposite)
    for dz in FAR:
        along_two(dz).start()
    spread_two(12, 4)
    spread_two(0, 5)
    met = [whole(p1.at[pl.ds(0, NZ * n)], p1.at[pl.ds(0, NZ * n)], xs, xr) for n in (7, 8)]

    @pl.when(alone)
    def _():
        met[0].wait_recv()

    @pl.when(jnp.logical_not(alone))
    def _():
        met[1].wait_recv()

    s1[...] = in1[0:4] + in1[4:8]
    pl.semaphore_wait(opposite_in, 1)
    for dz in FAR[:3] + NEAR + (0,) + FAR[3:]:
        along_one(dz).start()
    spread_two(7, 3)
    spread_two(5, 2)
    spread_two(10, 2)
    r2[pl.ds(yc * NZ, NZ)] = z2[:, yc]
    share(7, 3)
    share(12, 4)
    share(0, 5)
    share(5, 2)
    share(10, 2)

    for copy in loads[5:]:
        copy.wait()
    j = lax.broadcasted_iota(jnp.int32, (G, G), 1)
    hot2 = (((j // 32) * NZ + (z + j % NZ) % NZ) * 2 + (j // NZ) % 2 == i).astype(F32).astype(BF)
    hot1 = (((j % 4) * NZ + (z + (j // 4) % NZ) % NZ) * 2 + j // HALF == i).astype(F32).astype(BF)
    m2s = tuple(dot(v, hot2).astype(BF) for v in split(m2[...]))
    m1s = tuple(dot(v, hot1).astype(BF) for v in split(m1[...]))
    l2s, l1s = split(l2[...]), split(l1[...])

    rows2 = whole(r2.at[pl.ds(0, 7 * NZ)], r2.at[pl.ds(0, 7 * NZ)], send2, recv2)
    rows2.wait_recv()
    for k in (0, 2):
        rows = jnp.concatenate([r2[:, k, :], r2[:, k + 1, :]], 1)
        w2 = split(deep3(m2s, split(rows)))
        out[:, 128 * k : 128 * k + 256] = deep3(l2s, w2)
    shared = whole(r1.at[q], r1.at[q], fs, fr)
    shared.wait_recv()
    for k in (0, 2):
        rows = jnp.concatenate([r1[:, :, :, n, :].reshape(G, 128) for n in (k, k + 1)], 1)
        w1 = split(deep3(m1s, split(rows)))
        out[:, 128 * k : 128 * k + 256] += deep3(l1s, w1)
    whole(s2, s2, zs2, zr2.at[0]).wait_send()
    whole(r1.at[0], r1.at[0], zs1, zr1.at[0]).wait_send()

    @pl.when(alone)
    def _():
        met[0].wait_send()

    @pl.when(jnp.logical_not(alone))
    def _():
        met[1].wait_send()

    rows2.wait_send()
    shared.wait_send()


def on_device(rhs, left_one, left_two, middle_one, middle_two, right_one, right_two, order_one, order_two):
    dma = pltpu.SemaphoreType.DMA
    any_space = pl.BlockSpec(memory_space=pl.ANY)
    return pl.pallas_call(
        kernel,
        out_shape=pltpu.VMEM((256, 512), F32),
        in_specs=[any_space] * 9,
        out_specs=pl.BlockSpec(memory_space=pltpu.VMEM),
        scratch_shapes=[
            pltpu.VMEM((256, 512), F32),
            pltpu.VMEM((256, 128), F32),
            pltpu.VMEM((256, 128), F32),
            pltpu.VMEM((128, 128), F32),
            pltpu.VMEM((128, 128), F32),
            pltpu.VMEM((256, 128), F32),
            pltpu.VMEM((256, 128), F32),
            pltpu.VMEM((1, 128), jnp.int32),
            pltpu.VMEM((1, 128), jnp.int32),
            pltpu.VMEM((G, 4, 128), F32),
            pltpu.VMEM((G, 4, 128), F32),
            pltpu.VMEM((8, NZ, 4, 128), F32),
            pltpu.VMEM((4, NZ, 4, 128), F32),
            pltpu.VMEM((NZ, 8, 4, 128), F32),
            pltpu.VMEM((G, 4, 128), F32),
            pltpu.VMEM((2, NZ, 4, 4, 128), F32),
            dma((9,)), dma, dma((NZ,)), dma, dma, dma, dma((NZ,)), dma, dma, dma, dma,
            pltpu.SemaphoreType.REGULAR,
            pltpu.SemaphoreType.REGULAR,
        ],
        compiler_params=pltpu.CompilerParams(collective_id=0, has_side_effects=True),
        name="butterfly",
    )(rhs, left_one, left_two, middle_one, middle_two, right_one, right_two, order_one, order_two)


def solution(mesh):
    rows = P(("half", "quarter", "grp"), None)
    in_specs = (
        rows, rows, rows,
        P("half", "grp", None, None),
        P(("half", "quarter"), "grp", None, None),
        rows, rows,
        P("half", "grp", None),
        P(("half", "quarter"), "grp", None),
    )
    return jax.shard_map(on_device, mesh=mesh, in_specs=in_specs, out_specs=rows, check_vma=False)
```

```python
import functools

import jax
import jax.numpy as jnp
from jax import lax
from jax.experimental import pallas as pl
from jax.experimental.pallas import tpu as pltpu
from jax.sharding import PartitionSpec as P

MESH = pl.DeviceIdType.MESH
G = 128
HALF = 64
NZ = 16
NY = 4
BF = jnp.bfloat16
F32 = jnp.float32


def split(a):
    high = a.astype(BF)
    return high, (a - high.astype(F32)).astype(BF)


def dot(a, b, dims=(((1,), (0,)), ((), ()))):
    return lax.dot_general(a, b, dims, preferred_element_type=F32)


def dot3(a, b):
    (ah, al), (bh, bl) = a, b
    return dot(ah, bh) + (dot(ah, bl) + dot(al, bh))


def deep3(a, b):
    (ah, al), (bh, bl) = a, b
    return dot(jnp.concatenate([ah, al], 1), jnp.concatenate([bh, bh], 0)) + dot(ah, bl)


def permuted(factor, order, slot):
    hot = (order == slot).astype(F32).astype(BF)
    high, low = split(factor)
    nt = (((1,), (1,)), ((), ()))
    return dot(hot, high, nt).astype(BF), dot(hot, low, nt).astype(BF)


NEAR = (4, -4, 3, -3, 2, -2, 1, -1)
FAR = (8, 7, -7, 6, -6, 5, -5)


def kernel(
    x_hbm, l1_hbm, l2_hbm, m1_hbm, m2_hbm, rr1_hbm, rr2_hbm, o1_hbm, o2_hbm, out,
    x, l1, l2, m1, m2, rr1, rr2, o1, o2,
    s2, p1, in1, s1, z2, r2, r1,
    load_sem, zs2, zr2, xs, xr, zs1, zr1, send2, recv2, fs, fr, stage, opposite_in,
):
    h = lax.axis_index("half")
    q = lax.axis_index("quarter")
    me = lax.axis_index("grp")
    y, z, c = me // (2 * NZ), (me // 2) % NZ, me % 2
    yc = y * 2 + c

    loads = []
    for n, (a, b) in enumerate((
        (x_hbm, x), (rr2_hbm, rr2), (o2_hbm.at[0], o2), (rr1_hbm, rr1), (o1_hbm.at[0], o1),
        (m2_hbm.at[0, 0], m2), (m1_hbm.at[0, 0], m1), (l2_hbm, l2), (l1_hbm, l1),
    )):
        loads.append(pltpu.make_async_copy(a, b, load_sem.at[n]))

    def signal(semaphore, device):
        pl.semaphore_signal(semaphore, inc=1, device_id=device, device_id_type=MESH)

    def place(zz, t):
        return ((t // 2) * NZ + zz) * 2 + t % 2

    def level(dz):
        return (z + dz + NZ) % NZ

    def column(dz):
        return {"half": h, "quarter": q, "grp": place(level(dz), yc)}

    def sibling(dz):
        return {"half": h, "quarter": 1 - q, "grp": place(level(dz), yc)}

    across = {"half": h, "quarter": 1 - q, "grp": me}
    opposite = {"half": 1 - h, "quarter": q, "grp": me}

    loads[0].start()
    barrier = pltpu.get_barrier_semaphore()
    for dz in NEAR:
        signal(barrier, sibling(dz))
    for dz in (4, -4):
        signal(barrier, column(dz))
    signal(barrier, opposite)
    for s in range(1, 16):
        t = (yc * 2 + q + s) % 16
        signal(barrier, {"half": h, "quarter": t % 2, "grp": place(z, t // 2)})
    for copy in loads[1:]:
        copy.start()

    i = lax.broadcasted_iota(jnp.int32, (G, G), 0)
    slot2 = (((i // 2) % 4) * NZ + i // 8) * 2 + i % 2
    slot1 = ((i // 32) * NZ + i % NZ) * 2 + (i // NZ) % 2
    loads[0].wait()
    xs_ = split(x[...])
    loads[1].wait()
    loads[2].wait()
    c2 = dot3(permuted(rr2[...], o2[...], slot2), xs_)
    for k in range(4):
        s2[:, k, :] = c2[:, 128 * k : 128 * k + 128]
    loads[3].wait()
    loads[4].wait()
    c1 = dot3(permuted(rr1[...], o1[...], slot1), xs_)
    for k in range(4):
        p1[:, k, :] = c1[:, 128 * k : 128 * k + 128]

    def along_two(dz):
        return pltpu.make_async_remote_copy(
            s2.at[pl.ds(level(dz) * 8, 8)], z2.at[-dz % NZ], zs2, zr2.at[-dz % NZ],
            device_id=sibling(dz), device_id_type=MESH)

    def spread_two(first, count):
        for zi in range(first, first + count):
            along_two(-zi).wait_recv()

        def send(n, carry):
            t = (yc + n) % 8
            pltpu.make_async_remote_copy(
                z2.at[pl.ds(first, count), t], r2.at[pl.ds(yc * NZ + first, count)], send2, recv2,
                device_id={"half": h, "quarter": q, "grp": place(z, t)}, device_id_type=MESH).start()
            return carry

        lax.fori_loop(1, 8, send, 0)

    alone = c == q

    def spread_one(n, carry):
        t = (yc + n) % 8
        pltpu.make_async_remote_copy(
            p1.at[pl.ds(t * NZ, NZ)], in1.at[q * 4 + y], xs, xr,
            device_id={"half": h, "quarter": c, "grp": place(z, t)}, device_id_type=MESH).start()
        return carry

    def along_one(dz):
        return pltpu.make_async_remote_copy(
            s1.at[:, level(dz)], r1.at[q, -dz % NZ], zs1, zr1.at[-dz % NZ],
            device_id={"half": 1 - h, "quarter": 1 - q, "grp": place(level(dz), yc)},
            device_id_type=MESH)

    def whole(a, b, sent, received):
        return pltpu.make_async_remote_copy(a, b, sent, received, device_id=across, device_id_type=MESH)

    def share(first, count):
        for zi in range(first, first + count):
            row = r1.at[1 - q, zi]
            whole(row, row, zs1, zr1.at[zi]).wait_recv()
        rows = r1.at[1 - q, pl.ds(first, count)]
        whole(rows, rows, fs, fr).start()

    pl.semaphore_wait(barrier, 8 + 2 + 1 + 15)
    for dz in (4, -4):
        signal(stage, column(dz))

    @pl.when(jnp.logical_not(alone))
    def _():
        spread_one(0, 0)

    lax.fori_loop(1, 8, spread_one, 0)

    @pl.when(alone)
    def _():
        in1[q * 4 + y] = p1[pl.ds(yc * NZ, NZ)]

    for dz in NEAR + (0,):
        along_two(dz).start()
    pl.semaphore_wait(stage, 2)
    signal(opposite_in, opposite)
    for dz in FAR:
        along_two(dz).start()
    spread_two(12, 4)
    spread_two(0, 5)
    met = [whole(p1.at[pl.ds(0, NZ * n)], p1.at[pl.ds(0, NZ * n)], xs, xr) for n in (7, 8)]

    @pl.when(alone)
    def _():
        met[0].wait_recv()

    @pl.when(jnp.logical_not(alone))
    def _():
        met[1].wait_recv()

    s1[...] = in1[0:4] + in1[4:8]
    pl.semaphore_wait(opposite_in, 1)
    for dz in FAR[:3] + NEAR[4:] + (0,) + FAR[3:] + NEAR[:4]:
        along_one(dz).start()
    spread_two(7, 3)
    spread_two(5, 2)
    spread_two(10, 2)
    r2[pl.ds(yc * NZ, NZ)] = z2[:, yc]
    share(7, 3)
    share(14, 2)
    share(0, 3)
    share(5, 2)
    share(10, 2)
    share(12, 2)
    share(3, 2)

    for copy in loads[5:]:
        copy.wait()
    j = lax.broadcasted_iota(jnp.int32, (G, G), 1)
    hot2 = (((j // 32) * NZ + (z + j % NZ) % NZ) * 2 + (j // NZ) % 2 == i).astype(F32).astype(BF)
    hot1 = (((j % 4) * NZ + (z + (j // 4) % NZ) % NZ) * 2 + j // HALF == i).astype(F32).astype(BF)
    m2s = tuple(dot(v, hot2).astype(BF) for v in split(m2[...]))
    m1s = tuple(dot(v, hot1).astype(BF) for v in split(m1[...]))
    l2s, l1s = split(l2[...]), split(l1[...])

    rows2 = whole(r2.at[pl.ds(0, 7 * NZ)], r2.at[pl.ds(0, 7 * NZ)], send2, recv2)
    rows2.wait_recv()
    for k in (0, 2):
        rows = jnp.concatenate([r2[:, k, :], r2[:, k + 1, :]], 1)
        w2 = split(deep3(m2s, split(rows)))
        out[:, 128 * k : 128 * k + 256] = deep3(l2s, w2)
    shared = whole(r1.at[q], r1.at[q], fs, fr)
    shared.wait_recv()
    for k in (0, 2):
        rows = jnp.concatenate([r1[:, :, :, n, :].reshape(G, 128) for n in (k, k + 1)], 1)
        w1 = split(deep3(m1s, split(rows)))
        out[:, 128 * k : 128 * k + 256] += deep3(l1s, w1)
    whole(s2, s2, zs2, zr2.at[0]).wait_send()
    whole(r1.at[0], r1.at[0], zs1, zr1.at[0]).wait_send()

    @pl.when(alone)
    def _():
        met[0].wait_send()

    @pl.when(jnp.logical_not(alone))
    def _():
        met[1].wait_send()

    rows2.wait_send()
    shared.wait_send()


def on_device(rhs, left_one, left_two, middle_one, middle_two, right_one, right_two, order_one, order_two):
    dma = pltpu.SemaphoreType.DMA
    any_space = pl.BlockSpec(memory_space=pl.ANY)
    return pl.pallas_call(
        kernel,
        out_shape=pltpu.VMEM((256, 512), F32),
        in_specs=[any_space] * 9,
        out_specs=pl.BlockSpec(memory_space=pltpu.VMEM),
        scratch_shapes=[
            pltpu.VMEM((256, 512), F32),
            pltpu.VMEM((256, 128), F32),
            pltpu.VMEM((256, 128), F32),
            pltpu.VMEM((128, 128), F32),
            pltpu.VMEM((128, 128), F32),
            pltpu.VMEM((256, 128), F32),
            pltpu.VMEM((256, 128), F32),
            pltpu.VMEM((1, 128), jnp.int32),
            pltpu.VMEM((1, 128), jnp.int32),
            pltpu.VMEM((G, 4, 128), F32),
            pltpu.VMEM((G, 4, 128), F32),
            pltpu.VMEM((8, NZ, 4, 128), F32),
            pltpu.VMEM((4, NZ, 4, 128), F32),
            pltpu.VMEM((NZ, 8, 4, 128), F32),
            pltpu.VMEM((G, 4, 128), F32),
            pltpu.VMEM((2, NZ, 4, 4, 128), F32),
            dma((9,)), dma, dma((NZ,)), dma, dma, dma, dma((NZ,)), dma, dma, dma, dma,
            pltpu.SemaphoreType.REGULAR,
            pltpu.SemaphoreType.REGULAR,
        ],
        compiler_params=pltpu.CompilerParams(collective_id=0, has_side_effects=True),
        name="butterfly",
    )(rhs, left_one, left_two, middle_one, middle_two, right_one, right_two, order_one, order_two)


def solution(mesh):
    rows = P(("half", "quarter", "grp"), None)
    in_specs = (
        rows, rows, rows,
        P("half", "grp", None, None),
        P(("half", "quarter"), "grp", None, None),
        rows, rows,
        P("half", "grp", None),
        P(("half", "quarter"), "grp", None),
    )
    return jax.shard_map(on_device, mesh=mesh, in_specs=in_specs, out_specs=rows, check_vma=False)
```
